1024 devices in a mesh: section: 16 (over y, core), node: 4 (over x), local: 16 (over z).
Axes of the slice: x: 4, y: 8, z: 16, core: 2. Of those that a mesh axis runs over, the one named last changes fastest.
Arguments:
- tokens: bfloat16 [2, 3072, 7168], P(None, ('section', 'node', 'local')), may hold values from -6 to 6
- norm_gain: float32 [7168], replicated, may hold values from 0.1 to 1.9
- routes: int32 [2, 3072, 2], P(None, ('section', 'node', 'local')), may hold values from 0 to 3, all different within a row; in each aligned block of 3 rows (0 to 2, 3 to 5, ..., all dimensions but the last counted through in order) at most 2 rows name the same one
- gate_weight: float32 [2, 3072, 2], P(None, ('section', 'node', 'local')), may hold values from 0.25 to 1
- w_gate: bfloat16 [4, 7168, 2048], P('node', None, 'local'), may hold values from -0.0625 to 0.0625
- w_up: bfloat16 [4, 7168, 2048], P('node', None, 'local'), may hold values from -0.0625 to 0.0625
- w_down: bfloat16 [4, 2048, 7168], P('node', 'local'), may hold values from -0.125 to 0.125
Outputs:
- mixed_out: bfloat16 [2, 3072, 7168], P(None, ('section', 'node', 'local'))
The draws below stay inside these ranges and needn't reach their ends.
Inputs may be any that keep to these rules, and one draw needn't show every extreme that they name: `routes`: each row names 2 different experts. Among the 3 events of one device in one microbatch (an aligned block of rows), no expert is named more than 2 times, a bound that some block reaches.
All inputs are finite; a program needn't handle non-finite values.
Results may differ from the reference program's by a relative error of at most 0.011.
Values may be sent and summed in bfloat16 or wider, within the bound.
No kernel may reach another device: no remote copies, remote signals or barrier semaphores. Data moves between devices by JAX's collectives and lax.ppermute only.
A program may use at most 32 MiB of HBM per device.

```python
import math
import jax
import jax.numpy as jnp
import numpy as np
from jax import lax

D = 7168
FF = 2048
TOP = 2
MICRO = 2
TOK_DEV = 3
EXPERTS = 4
CAP = 2
EVENTS = 3072
N_SECTION = 16
N_LOCAL = 16


def levels(key, dims, split, low, high):
    factor_of = 1.0
    for dim, parts in split:
        steps = jax.random.uniform(jax.random.fold_in(jax.random.fold_in(key, 6), dim), (parts,), jnp.float32, low / len(split), high / len(split))
        factor_of = factor_of * jnp.repeat(jnp.exp(steps), dims[dim] // parts).reshape((-1,) + (1,) * (len(dims) - 1 - dim))
    return factor_of


def shared_out(stream_key, own, number, rows, count, top, bound, slope):
    sequence = jax.random.permutation(stream_key, count)
    heavy_load, common = load_shares(count, rows * top, bound, slope, True), load_shares(count, rows * top, bound, slope, False)
    places = jnp.arange(count)

    def named(lengths, rotation):
        used = int((lengths > 0).sum())
        fixed = max(1, used // 4)
        passed = fixed + (places - fixed + rotation * (used - fixed)) % max(1, count - fixed)
        return jnp.zeros((count,), jnp.int32).at[sequence[jnp.where(places < fixed, places, passed)]].set(jnp.asarray(lengths, jnp.int32))

    lengths = jnp.where(number % 4 == 0, named(heavy_load, number // 4), named(common, number - number // 4 - 1))
    mixed = jax.random.permutation(jax.random.fold_in(own, 3), count)
    giver, receiver = mixed[0:count // 2 * 2:2], mixed[1:count // 2 * 2:2]
    slack = jnp.minimum(lengths[giver] - 1, bound - lengths[receiver]) // 2
    slack = jnp.where((giver == sequence[0]) | (receiver == sequence[0]) | (lengths[receiver] == 0), 0, jnp.maximum(slack, 0))
    passed = jax.random.randint(jax.random.fold_in(own, 4), (count // 2,), 0, 1 << 20) % (slack + 1)
    lengths = lengths.at[giver].add(-passed).at[receiver].add(passed)
    labels = jnp.searchsorted(jnp.cumsum(lengths), jnp.arange(rows * top), side="right").astype(jnp.int32)
    grid = labels.reshape(top, rows).T
    grid = grid[jax.random.permutation(jax.random.fold_in(own, 1), rows)]
    rotation = jax.random.randint(jax.random.fold_in(own, 2), (rows, 1), 0, top)
    return jnp.take_along_axis(grid, (jnp.arange(top)[None, :] + rotation) % top, axis=1)


def load_shares(number_of, total, reach, lean, full):
    weights = [(1 << 20) // math.isqrt(grade ** lean) + 1 for grade in range(1, number_of + 1)]
    largest = reach if full else min(reach, max(-(-total // number_of), total * weights[0] // sum(weights)))
    least = 1 if total - largest >= number_of - 1 else 0
    counts, rest = [largest] + [least] * (number_of - 1), total - largest - least * (number_of - 1)
    while rest > 0:
        movable = [i for i in range(1, number_of) if counts[i] < largest] or [i for i in range(1, number_of) if counts[i] < reach]
        mass, remaining = sum([weights[i] for i in movable]), rest
        for i in movable:
            more = min(reach - counts[i], max(1, remaining * weights[i] // mass), rest)
            counts[i] = counts[i] + more
            rest = rest - more
    return np.array(counts)


def gaussian(rng, shape, deviation, reach, cuts=(), held_as=jnp.bfloat16):
    result = deviation * jax.random.normal(rng, shape, jnp.float32)
    if cuts:
        result = result * levels(rng, shape, cuts, -0.22, 0.18)
    return jnp.clip(result, -reach, reach).astype(held_as)


def setup_inputs(seed: int = 0) -> dict:
    streams_of = jax.random.split(jax.random.key(seed), 8)
    tokens = gaussian(streams_of[0], (MICRO, EVENTS, D), 1.0, 6.0, ((1, 1024),))
    norm_gain = jnp.clip(1.0 + 0.18 * jax.random.normal(streams_of[1], (D,), jnp.float32), 0.1, 1.9)
    routes_keys = jax.random.split(jax.random.fold_in(streams_of[2], 1), MICRO * EVENTS // TOK_DEV)
    routes_turns = jax.random.permutation(jax.random.fold_in(streams_of[2], 3), MICRO * EVENTS // TOK_DEV)
    routes = jax.vmap(lambda own, number: shared_out(jax.random.fold_in(streams_of[2], 2), own, number, TOK_DEV, EXPERTS, TOP, CAP, 2))(routes_keys, routes_turns).reshape((MICRO, EVENTS, TOP))
    gate_weight = jnp.clip(0.25 + 0.75 * jax.random.uniform(streams_of[3], (MICRO, EVENTS, TOP), jnp.float32) ** levels(streams_of[3], (MICRO, EVENTS, TOP), ((1, 1024),), -0.2, 0.2), 0.25, 1.0)
    w_gate = gaussian(streams_of[4], (EXPERTS, D, FF), D ** -0.5, 0.0625, ((0, 4), (2, 16)))
    w_up = gaussian(streams_of[5], (EXPERTS, D, FF), D ** -0.5, 0.0625, ((0, 4), (2, 16)))
    w_down = gaussian(streams_of[6], (EXPERTS, FF, D), FF ** -0.5, 0.125, ((0, 4), (1, 16)))
    return {"tokens": tokens, "norm_gain": norm_gain, "routes": routes, "gate_weight": gate_weight, "w_gate": w_gate, "w_up": w_up, "w_down": w_down}


def reference(tokens, norm_gain, routes, gate_weight, w_gate, w_up, w_down):
    per_section = EVENTS // N_SECTION
    arrived = jnp.roll(tokens.reshape(MICRO, N_SECTION, per_section, D), 1, axis=1).reshape(MICRO * EVENTS, D)
    wide = arrived.astype(jnp.float32)
    mean_square = lax.optimization_barrier(jnp.mean(wide * wide, axis=1, keepdims=True))
    normed = (wide * lax.rsqrt(mean_square + 1e-06) * norm_gain).astype(jnp.bfloat16)
    blocks = MICRO * EVENTS // TOK_DEV
    block_routes = routes.reshape(blocks, TOK_DEV, TOP).astype(jnp.int32)
    block_gates = gate_weight.reshape(blocks, TOK_DEV, TOP).astype(jnp.float32)
    capacity_rows = blocks * CAP
    hid_dev = FF // N_LOCAL
    source_index = jnp.arange(blocks * TOK_DEV, dtype=jnp.int32).reshape(blocks, TOK_DEV)
    block_base = (jnp.arange(blocks, dtype=jnp.int32) * CAP)[:, None]

    def one_expert(expert, mixed_sum):
        chosen = block_routes == expert
        picked = lax.optimization_barrier(jnp.sum(chosen.astype(jnp.int32), axis=2))
        weight = lax.optimization_barrier(jnp.sum(jnp.where(chosen, block_gates, jnp.float32(0.0)), axis=2))
        slot_rank = jnp.cumsum(picked, axis=1).astype(jnp.int32) - 1
        slot = jnp.where(picked > 0, block_base + slot_rank, capacity_rows).astype(jnp.int32)
        slot_source = jnp.zeros((capacity_rows + 1,), jnp.int32).at[slot.reshape(-1)].set(source_index.reshape(-1))
        row_data = normed[slot_source[:capacity_rows]]
        gate_act = jnp.dot(row_data, w_gate[expert], preferred_element_type=jnp.float32)
        up_act = jnp.dot(row_data, w_up[expert], preferred_element_type=jnp.float32)
        hidden = (jax.nn.silu(gate_act) * up_act).astype(jnp.bfloat16)
        hidden_blocks = jnp.swapaxes(hidden.reshape(capacity_rows, N_LOCAL, hid_dev), 0, 1)
        down_blocks = w_down[expert].reshape(N_LOCAL, hid_dev, D)

        def add_block(partial_sum, pair):
            block_hidden, block_down = pair
            product = jnp.dot(block_hidden, block_down, preferred_element_type=jnp.float32).astype(jnp.bfloat16)
            product = lax.optimization_barrier(product)
            return (partial_sum + product.astype(jnp.float32), None)
        summed = lax.scan(add_block, jnp.zeros((capacity_rows, D), jnp.float32), (hidden_blocks, down_blocks))[0]
        expert_out = jnp.concatenate([summed.astype(jnp.bfloat16), jnp.zeros((1, D), jnp.bfloat16)], axis=0)
        taken = expert_out[slot.reshape(-1)].astype(jnp.float32)
        return mixed_sum + weight.reshape(-1, 1) * taken
    mixed_sum = lax.fori_loop(0, EXPERTS, one_expert, jnp.zeros((MICRO * EVENTS, D), jnp.float32))
    mixed_out = (wide + mixed_sum).astype(jnp.bfloat16)
    return mixed_out.reshape(MICRO, EVENTS, D)
```

```python
import functools

import jax
import jax.numpy as jnp
from jax import lax
from jax.experimental import pallas as pl
from jax.experimental.pallas import tpu as pltpu
from jax.sharding import Mesh
from jax.sharding import PartitionSpec as P

F32 = jnp.float32
BF16 = jnp.bfloat16


def ring(value, step):
    count = lax.axis_size("local")
    pairs = []
    for core, sign in ((0, step), (1, -step)):
        for z in range(count):
            pairs.append((core * count + z, core * count + (z + sign) % count))
    return lax.ppermute(value, ("core", "local"), pairs)


def expert_body(*refs, count):
    pieces, (gate_ref, up_ref, down_ref), outs = refs[:count], refs[count : count + 3], refs[count + 3 :]
    rows, width = pieces[0].shape
    hidden = gate_ref.shape[1]
    gate = jnp.zeros((count * rows, hidden), F32)
    up = jnp.zeros((count * rows, hidden), F32)
    block = 1024
    for start in range(0, width, block):
        stop = start + block
        x = jnp.concatenate([p[:, start:stop] for p in pieces], axis=0)
        gate = gate + jnp.dot(x, gate_ref[start:stop, :], preferred_element_type=F32)
        up = up + jnp.dot(x, up_ref[start:stop, :], preferred_element_type=F32)
    act = (gate / (1.0 + jnp.exp(-gate)) * up).astype(BF16)
    block = 512
    for start in range(0, width, block):
        stop = start + block
        y = jnp.dot(act, down_ref[:, start:stop], preferred_element_type=F32).astype(BF16)
        for i, out in enumerate(outs):
            out[:, start:stop] = y[i * rows : (i + 1) * rows]


def experts(pieces, w_gate, w_up, w_down):
    count = len(pieces)
    vmem = pl.BlockSpec(memory_space=pltpu.VMEM)
    shape = jax.ShapeDtypeStruct(pieces[0].shape, BF16)
    call = pl.pallas_call(
        functools.partial(expert_body, count=count),
        out_shape=[shape] * count,
        in_specs=[vmem] * (count + 3),
        out_specs=[vmem] * count,
        compiler_params=pltpu.CompilerParams(vmem_limit_bytes=32 << 20),
    )
    return list(call(*pieces, w_gate, w_up, w_down))


def join_body(a_ref, b_ref, o_ref):
    o_ref[...] = (a_ref[...].astype(F32) + b_ref[...].astype(F32)).astype(BF16)


def join_kernel(a, b):
    vmem = pl.BlockSpec(memory_space=pltpu.VMEM)
    return pl.pallas_call(
        join_body,
        out_shape=jax.ShapeDtypeStruct(a.shape, BF16),
        in_specs=[vmem, vmem],
        out_specs=vmem,
        compiler_params=pltpu.CompilerParams(vmem_limit_bytes=8 << 20),
    )(a, b)


def shards(tokens, norm_gain, routes, gate_weight, w_gate, w_up, w_down):
    micro, events, width = tokens.shape
    groups = lax.axis_size("node")
    cores = lax.axis_size("core")
    ring_len = lax.axis_size("local")
    sections = lax.axis_size("y") * cores
    total = micro * events
    top = routes.shape[2]
    capacity = min(events, max(2, (events * top + groups - 1) // groups))
    dests = groups * cores
    slots = dests * micro * capacity

    pairs = [(s, (s + 1) % sections) for s in range(sections)]
    arrived = lax.ppermute(tokens, ("y", "core"), pairs)
    wide = arrived.astype(F32)
    mean_square = jnp.mean(wide * wide, axis=2, keepdims=True)
    normed = (wide * lax.rsqrt(mean_square + 1e-06) * norm_gain).astype(BF16)

    chosen = routes[:, :, :, None] == jnp.arange(groups, dtype=jnp.int32)
    picked = jnp.sum(chosen.astype(jnp.int32), axis=2)
    weight = jnp.sum(jnp.where(chosen, gate_weight[:, :, :, None], 0.0), axis=2)
    slot_rank = jnp.cumsum(picked, axis=1) - 1
    placed = (picked[..., None] > 0) & (
        slot_rank[..., None] == jnp.arange(capacity, dtype=jnp.int32)
    )
    ids = jnp.arange(micro)
    want = ids[None, :] ^ ids[:cores, None]
    match = want[:, :, None] == ids
    place = placed[None, None].astype(F32) * match[:, :, :, None, None, None].astype(F32)
    place = jnp.transpose(place, (4, 0, 1, 5, 2, 3)).reshape(slots, total)
    spread = jnp.transpose(weight, (2, 0, 1)).reshape(groups, 1, total)
    mix = (place.reshape(groups, slots // groups, total) * spread).reshape(slots, total)

    sent = jnp.dot(place.astype(BF16), normed.reshape(total, width), preferred_element_type=F32)
    sent = sent.astype(BF16).reshape(dests, slots // dests, width)
    got = lax.all_to_all(sent, ("node", "core"), split_axis=0, concat_axis=0, tiled=True)
    got = got.reshape(dests, micro, capacity, width)
    rows = dests * capacity
    chains = [[got[:, o].reshape(rows, width)] for o in range(micro)]
    half = ring_len // 2
    for hop in range(half):
        chains[0].append(ring(chains[0][-1], 1))
        if hop < half - 1:
            chains[1].append(ring(chains[1][-1], 1))

    weights = (w_gate[0], w_up[0], w_down[0])
    first, second = chains
    parts = experts(first[:half] + second[1:half], *weights)
    part_first, part_second = parts[:half], [None] + parts[half:]
    part_first = part_first + experts([first[half]], *weights)

    acc_second = part_second[half - 1]
    acc_first = part_first[half]
    for hop in range(half - 1, -1, -1):
        if hop > 0:
            acc_second = ring(acc_second, -1)
            if hop > 1:
                acc_second = join_kernel(acc_second, part_second[hop - 1])
        acc_first = ring(acc_first, -1)
        acc_first = (acc_first.astype(F32) + part_first[hop].astype(F32)).astype(BF16)

    back = jnp.stack(
        [acc_first.reshape(dests, capacity, width), acc_second.reshape(dests, capacity, width)],
        axis=1,
    ).reshape(dests, micro * capacity, width)
    back = lax.all_to_all(back, ("node", "core"), split_axis=0, concat_axis=0, tiled=True)
    mixed = lax.dot_general(
        mix,
        back.reshape(slots, width).astype(F32),
        (((0,), (0,)), ((), ())),
        precision=lax.Precision.HIGHEST,
        preferred_element_type=F32,
    )
    return (wide + mixed.reshape(micro, events, width)).astype(BF16)


def solution(mesh):
    sections, nodes, locals_ = mesh.devices.shape
    split = Mesh(
        mesh.devices.reshape(sections // 2, 2, nodes, locals_),
        ("y", "core", "node", "local"),
    )
    spread = ("y", "core", "node", "local")
    placed = (
        P(None, spread, None),
        P(),
        P(None, spread, None),
        P(None, spread, None),
        P("node", None, "local"),
        P("node", None, "local"),
        P("node", "local", None),
    )
    return jax.shard_map(
        shards,
        mesh=split,
        in_specs=placed,
        out_specs=P(None, spread, None),
        check_vma=False,
    )
```

```python
import functools

import jax
import jax.numpy as jnp
from jax import lax
from jax.experimental import pallas as pl
from jax.experimental.pallas import tpu as pltpu
from jax.sharding import Mesh
from jax.sharding import PartitionSpec as P

F32 = jnp.float32
BF16 = jnp.bfloat16


def ring(value, step, hop):
    count = lax.axis_size("local")
    pairs = []
    for core, sign in ((0, step), (1, -step)):
        if hop > (count - 1 + core) // 2:
            continue
        for z in range(count):
            pairs.append((core * count + z, core * count + (z + sign) % count))
    return lax.ppermute(value, ("core", "local"), pairs)


def expert_body(*refs, count, block):
    pieces, gate_ref, weights = refs[:count], refs[count], refs[count + 1 : count + 3]
    outs, (up_ref, down_ref, up_sem, down_sem) = refs[count + 3 : 2 * count + 3], refs[2 * count + 3 :]
    rows, width = pieces[0].shape
    hidden = gate_ref.shape[1]
    starts = range(0, width, block)

    def up_copy(i):
        part = pl.ds(i * block, block)
        return pltpu.make_async_copy(weights[0].at[part], up_ref.at[part], up_sem.at[i])

    down_copy = pltpu.make_async_copy(weights[1], down_ref, down_sem)
    for i in range(len(starts)):
        up_copy(i).start()
    down_copy.start()

    def project(weight_ref, wait):
        total = jnp.zeros((count * rows, hidden), F32)
        for i, start in enumerate(starts):
            stop = start + block
            wait(i)
            x = jnp.concatenate([p[:, start:stop] for p in pieces], axis=0)
            total = total + jnp.dot(x, weight_ref[start:stop, :], preferred_element_type=F32)
        return total

    gate = project(gate_ref, lambda i: None)
    up = project(up_ref, lambda i: up_copy(i).wait())
    act = (gate / (1.0 + jnp.exp(-gate)) * up).astype(BF16)
    down_copy.wait()
    step = 512
    for start in range(0, width, step):
        stop = start + step
        y = jnp.dot(act, down_ref[:, start:stop], preferred_element_type=F32).astype(BF16)
        for i, out in enumerate(outs):
            out[:, start:stop] = y[i * rows : (i + 1) * rows]


def experts(pieces, w_gate, w_up, w_down):
    count = len(pieces)
    block = 1024
    vmem = pl.BlockSpec(memory_space=pltpu.VMEM)
    held = [pltpu.with_memory_space_constraint(w, pltpu.HBM) for w in (w_up, w_down)]
    call = pl.pallas_call(
        functools.partial(expert_body, count=count, block=block),
        out_shape=[jax.ShapeDtypeStruct(pieces[0].shape, BF16)] * count,
        in_specs=[vmem] * (count + 1) + [pl.BlockSpec(memory_space=pltpu.HBM)] * 2,
        out_specs=[vmem] * count,
        scratch_shapes=[
            pltpu.VMEM(w_up.shape, BF16),
            pltpu.VMEM(w_down.shape, BF16),
            pltpu.SemaphoreType.DMA((w_up.shape[0] // block,)),
            pltpu.SemaphoreType.DMA,
        ],
        compiler_params=pltpu.CompilerParams(vmem_limit_bytes=32 << 20),
    )
    return list(call(*pieces, w_gate, *held))


def join_body(a_ref, b_ref, o_ref):
    o_ref[...] = (a_ref[...].astype(F32) + b_ref[...].astype(F32)).astype(BF16)


def join_kernel(a, b):
    vmem = pl.BlockSpec(memory_space=pltpu.VMEM)
    return pl.pallas_call(
        join_body,
        out_shape=jax.ShapeDtypeStruct(a.shape, BF16),
        in_specs=[vmem, vmem],
        out_specs=vmem,
        compiler_params=pltpu.CompilerParams(vmem_limit_bytes=8 << 20),
    )(a, b)


def shards(tokens, norm_gain, routes, gate_weight, w_gate, w_up, w_down):
    micro, events, width = tokens.shape
    groups = lax.axis_size("node")
    cores = lax.axis_size("core")
    ring_len = lax.axis_size("local")
    sections = lax.axis_size("y") * cores
    total = micro * events
    top = routes.shape[2]
    capacity = min(events, max(2, (events * top + groups - 1) // groups))
    dests = groups * cores
    rows = dests * capacity
    half = ring_len // 2

    pairs = [(s, (s + 1) % sections) for s in range(sections)]
    arrived = lax.ppermute(jnp.transpose(tokens, (1, 0, 2)), ("y", "core"), pairs)
    wide = arrived.astype(F32)
    mean_square = jnp.mean(wide * wide, axis=2, keepdims=True)
    normed = (wide * lax.rsqrt(mean_square + 1e-06) * norm_gain).astype(BF16)
    normed = normed.reshape(total, width)

    chosen = routes[:, :, :, None] == jnp.arange(groups, dtype=jnp.int32)
    picked = jnp.sum(chosen.astype(jnp.int32), axis=2)
    weight = jnp.sum(jnp.where(chosen, gate_weight[:, :, :, None], 0.0), axis=2)
    slot_rank = jnp.cumsum(picked, axis=1) - 1
    placed = (picked[..., None] > 0) & (
        slot_rank[..., None] == jnp.arange(capacity, dtype=jnp.int32)
    )
    ids = jnp.arange(micro)
    want = ids[None, :] ^ ids[:cores, None]
    match = want[:, :, None] == ids
    place = placed[None, None].astype(F32) * match[:, :, :, None, None, None].astype(F32)
    mix = place * weight[None, None, :, :, :, None]
    slots = rows * micro
    place = jnp.transpose(place, (4, 0, 1, 5, 3, 2)).reshape(slots, total)
    mix = jnp.transpose(mix, (4, 0, 1, 5, 3, 2)).reshape(slots, total)

    def exchange(value):
        value = value.reshape(dests, micro * capacity, width)
        return lax.all_to_all(value, ("node", "core"), split_axis=0, concat_axis=0, tiled=True)

    sent = jnp.dot(place.astype(BF16), normed, preferred_element_type=F32)
    got = exchange(sent.astype(BF16)).reshape(dests, micro, capacity, width)
    chains = [[got[:, o].reshape(rows, width)] for o in range(micro)]
    for hop in range(1, half + 1):
        for chain in chains:
            chain.append(ring(chain[-1], 1, hop))

    first, second = chains
    parts = experts(first + second[1:], w_gate[0], w_up[0], w_down[0])
    part_first, part_second = parts[: half + 1], [None] + parts[half + 1 :]

    acc_first, acc_second = part_first[half], part_second[half]
    for hop in range(half, 0, -1):
        acc_first = ring(acc_first, -1, hop)
        acc_first = (acc_first.astype(F32) + part_first[hop - 1].astype(F32)).astype(BF16)
        acc_second = ring(acc_second, -1, hop)
        if hop > 1:
            acc_second = join_kernel(acc_second, part_second[hop - 1])

    back = jnp.stack(
        [acc_first.reshape(dests, capacity, width), acc_second.reshape(dests, capacity, width)],
        axis=1,
    )
    mixed = lax.dot_general(
        mix,
        exchange(back).reshape(slots, width).astype(F32),
        (((0,), (0,)), ((), ())),
        precision=lax.Precision.HIGHEST,
        preferred_element_type=F32,
    )
    mixed = (wide.reshape(total, width) + mixed).astype(BF16)
    return jnp.transpose(mixed.reshape(events, micro, width), (1, 0, 2))


def solution(mesh):
    sections, nodes, locals_ = mesh.devices.shape
    split = Mesh(
        mesh.devices.reshape(sections // 2, 2, nodes, locals_),
        ("y", "core", "node", "local"),
    )
    spread = ("y", "core", "node", "local")
    placed = (
        P(None, spread, None),
        P(),
        P(None, spread, None),
        P(None, spread, None),
        P("node", None, "local"),
        P("node", None, "local"),
        P("node", "local", None),
    )
    return jax.shard_map(
        shards,
        mesh=split,
        in_specs=placed,
        out_specs=P(None, spread, None),
        check_vma=False,
    )
```

```python
import functools

import jax
import jax.numpy as jnp
from jax import lax
from jax.experimental import pallas as pl
from jax.experimental.pallas import tpu as pltpu
from jax.sharding import Mesh
from jax.sharding import PartitionSpec as P

F32 = jnp.float32
BF16 = jnp.bfloat16


def ring(value, step, hop):
    count = lax.axis_size("local")
    pairs = []
    for core, sign in ((0, step), (1, -step)):
        if hop > (count - 1 + core) // 2:
            continue
        for z in range(count):
            pairs.append((core * count + z, core * count + (z + sign) % count))
    return lax.ppermute(value, ("core", "local"), pairs)


def hidden_body(*refs, count, block):
    pieces, (gate_ref, weight, act_ref, up_ref, sem) = refs[:count], refs[count:]
    rows, width = pieces[0].shape
    hidden = gate_ref.shape[1]
    starts = range(0, width, block)

    def up_copy(i):
        part = pl.ds(i * block, block)
        return pltpu.make_async_copy(weight.at[part], up_ref.at[part], sem.at[i])

    for i in range(len(starts)):
        up_copy(i).start()

    gate = jnp.zeros((count * rows, hidden), F32)
    up = jnp.zeros((count * rows, hidden), F32)
    for i, start in enumerate(starts):
        stop = start + block
        x = jnp.concatenate([p[:, start:stop] for p in pieces], axis=0)
        up_copy(i).wait()
        gate = gate + jnp.dot(x, gate_ref[start:stop, :], preferred_element_type=F32)
        up = up + jnp.dot(x, up_ref[start:stop, :], preferred_element_type=F32)
    act_ref[...] = (gate / (1.0 + jnp.exp(-gate)) * up).astype(BF16)


def down_body(act_ref, down_ref, *outs):
    rows, width = outs[0].shape
    act = act_ref[...]
    step = 512
    for start in range(0, width, step):
        stop = start + step
        y = jnp.dot(act, down_ref[:, start:stop], preferred_element_type=F32).astype(BF16)
        for i, out in enumerate(outs):
            out[:, start:stop] = y[i * rows : (i + 1) * rows]


def experts(pieces, w_gate, w_up, w_down):
    count = len(pieces)
    rows, width = pieces[0].shape
    hidden = w_gate.shape[1]
    block = width // 7
    vmem = pl.BlockSpec(memory_space=pltpu.VMEM)
    act = pl.pallas_call(
        functools.partial(hidden_body, count=count, block=block),
        out_shape=jax.ShapeDtypeStruct((count * rows, hidden), BF16),
        in_specs=[vmem] * (count + 1) + [pl.BlockSpec(memory_space=pltpu.HBM)],
        out_specs=vmem,
        scratch_shapes=[pltpu.VMEM(w_up.shape, BF16), pltpu.SemaphoreType.DMA((width // block,))],
        compiler_params=pltpu.CompilerParams(vmem_limit_bytes=24 << 20),
    )(*pieces, w_gate, pltpu.with_memory_space_constraint(w_up, pltpu.HBM))
    outs = pl.pallas_call(
        down_body,
        out_shape=[jax.ShapeDtypeStruct((rows, width), BF16)] * count,
        in_specs=[vmem] * 2,
        out_specs=[vmem] * count,
        compiler_params=pltpu.CompilerParams(vmem_limit_bytes=24 << 20),
    )(act, w_down)
    return list(outs)


def join_body(a_ref, b_ref, o_ref):
    o_ref[...] = (a_ref[...].astype(F32) + b_ref[...].astype(F32)).astype(BF16)


def join_kernel(a, b):
    vmem = pl.BlockSpec(memory_space=pltpu.VMEM)
    return pl.pallas_call(
        join_body,
        out_shape=jax.ShapeDtypeStruct(a.shape, BF16),
        in_specs=[vmem, vmem],
        out_specs=vmem,
        compiler_params=pltpu.CompilerParams(vmem_limit_bytes=8 << 20),
    )(a, b)


def shards(tokens, norm_gain, routes, gate_weight, w_gate, w_up, w_down):
    micro, events, width = tokens.shape
    groups = lax.axis_size("node")
    cores = lax.axis_size("core")
    ring_len = lax.axis_size("local")
    sections = lax.axis_size("y") * cores
    total = micro * events
    top = routes.shape[2]
    capacity = min(events, max(2, (events * top + groups - 1) // groups))
    dests = groups * cores
    rows = dests * capacity
    half = ring_len // 2

    pairs = [(s, (s + 1) % sections) for s in range(sections)]
    arrived = lax.ppermute(jnp.transpose(tokens, (1, 0, 2)), ("y", "core"), pairs)
    wide = arrived.astype(F32)
    mean_square = jnp.mean(wide * wide, axis=2, keepdims=True)
    normed = (wide * lax.rsqrt(mean_square + 1e-06) * norm_gain).astype(BF16)
    normed = normed.reshape(total, width)

    chosen = routes[:, :, :, None] == jnp.arange(groups, dtype=jnp.int32)
    picked = jnp.sum(chosen.astype(jnp.int32), axis=2)
    weight = jnp.sum(jnp.where(chosen, gate_weight[:, :, :, None], 0.0), axis=2)
    slot_rank = jnp.cumsum(picked, axis=1) - 1
    placed = (picked[..., None] > 0) & (
        slot_rank[..., None] == jnp.arange(capacity, dtype=jnp.int32)
    )
    ids = jnp.arange(micro)
    want = ids[None, :] ^ ids[:cores, None]
    match = want[:, :, None] == ids
    place = placed[None, None].astype(F32) * match[:, :, :, None, None, None].astype(F32)
    mix = place * weight[None, None, :, :, :, None]
    slots = rows * micro
    place = jnp.transpose(place, (4, 0, 1, 5, 3, 2)).reshape(slots, total)
    mix = jnp.transpose(mix, (4, 0, 1, 5, 3, 2)).reshape(slots, total)

    def exchange(value):
        value = value.reshape(dests, micro * capacity, width)
        return lax.all_to_all(value, ("node", "core"), split_axis=0, concat_axis=0, tiled=True)

    sent = jnp.dot(place.astype(BF16), normed, preferred_element_type=F32)
    got = exchange(sent.astype(BF16)).reshape(dests, micro, capacity, width)
    chains = [[got[:, o].reshape(rows, width)] for o in range(micro)]
    for hop in range(1, half + 1):
        for chain in chains:
            chain.append(ring(chain[-1], 1, hop))

    first, second = chains
    parts = experts(first + second[1:], w_gate[0], w_up[0], w_down[0])
    part_first, part_second = parts[: half + 1], [None] + parts[half + 1 :]

    acc_first, acc_second = part_first[half], part_second[half]
    for hop in range(half, 0, -1):
        acc_first = ring(acc_first, -1, hop)
        acc_first = (acc_first.astype(F32) + part_first[hop - 1].astype(F32)).astype(BF16)
        acc_second = ring(acc_second, -1, hop)
        if hop > 1:
            acc_second = join_kernel(acc_second, part_second[hop - 1])

    back = jnp.stack(
        [acc_first.reshape(dests, capacity, width), acc_second.reshape(dests, capacity, width)],
        axis=1,
    )
    mixed = lax.dot_general(
        mix,
        exchange(back).reshape(slots, width).astype(F32),
        (((0,), (0,)), ((), ())),
        precision=lax.Precision.HIGHEST,
        preferred_element_type=F32,
    )
    mixed = (wide.reshape(total, width) + mixed).astype(BF16)
    return jnp.transpose(mixed.reshape(events, micro, width), (1, 0, 2))


def solution(mesh):
    sections, nodes, locals_ = mesh.devices.shape
    split = Mesh(
        mesh.devices.reshape(sections // 2, 2, nodes, locals_),
        ("y", "core", "node", "local"),
    )
    spread = ("y", "core", "node", "local")
    placed = (
        P(None, spread, None),
        P(),
        P(None, spread, None),
        P(None, spread, None),
        P("node", None, "local"),
        P("node", None, "local"),
        P("node", "local", None),
    )
    return jax.shard_map(
        shards,
        mesh=split,
        in_specs=placed,
        out_specs=P(None, spread, None),
        check_vma=False,
    )
```

```python
import functools

import jax
import jax.numpy as jnp
from jax import lax
from jax.experimental import pallas as pl
from jax.experimental.pallas import tpu as pltpu
from jax.sharding import Mesh
from jax.sharding import PartitionSpec as P

F32 = jnp.float32
BF16 = jnp.bfloat16


def pack_body(a_ref, b_ref, c_ref, o_ref):
    first = a_ref[...].astype(F32) + b_ref[...].astype(F32)
    second = c_ref[...].astype(F32)
    dests, held, _ = o_ref.shape
    half = held // 2
    for i in range(dests):
        rows = slice(i * half, (i + 1) * half)
        both = jnp.concatenate([first[rows], second[rows]], axis=0)
        o_ref[i] = both.astype(BF16)


def pack(a, b, c, dests):
    vmem = pl.BlockSpec(memory_space=pltpu.VMEM)
    return pl.pallas_call(
        pack_body,
        out_shape=jax.ShapeDtypeStruct((dests, 2 * a.shape[0] // dests, a.shape[1]), BF16),
        in_specs=[vmem] * 3,
        out_specs=vmem,
        compiler_params=pltpu.CompilerParams(vmem_limit_bytes=8 << 20),
    )(a, b, c)


def ring(value, step, hop):
    count = lax.axis_size("local")
    pairs = []
    for core, sign in ((0, step), (1, -step)):
        if hop > (count - 1 + core) // 2:
            continue
        for z in range(count):
            pairs.append((core * count + z, core * count + (z + sign) % count))
    return lax.ppermute(value, ("core", "local"), pairs)


def hidden_body(*refs, count, block):
    pieces, (gate_ref, weight, act_ref, up_ref, sem) = refs[:count], refs[count:]
    rows, width = pieces[0].shape
    hidden = gate_ref.shape[1]
    starts = range(0, width, block)

    def up_copy(i):
        part = pl.ds(i * block, block)
        return pltpu.make_async_copy(weight.at[part], up_ref.at[part], sem.at[i])

    for i in range(len(starts)):
        up_copy(i).start()

    gate = jnp.zeros((count * rows, hidden), F32)
    up = jnp.zeros((count * rows, hidden), F32)
    for i, start in enumerate(starts):
        stop = start + block
        x = jnp.concatenate([p[:, start:stop] for p in pieces], axis=0)
        up_copy(i).wait()
        gate = gate + jnp.dot(x, gate_ref[start:stop, :], preferred_element_type=F32)
        up = up + jnp.dot(x, up_ref[start:stop, :], preferred_element_type=F32)
    act_ref[...] = (gate / (1.0 + jnp.exp(-gate)) * up).astype(BF16)


def down_body(act_ref, down_ref, *outs):
    rows, width = outs[0].shape
    act = act_ref[...]
    step = 512
    for start in range(0, width, step):
        stop = start + step
        y = jnp.dot(act, down_ref[:, start:stop], preferred_element_type=F32).astype(BF16)
        for i, out in enumerate(outs):
            out[:, start:stop] = y[i * rows : (i + 1) * rows]


def experts(pieces, w_gate, w_up, w_down):
    count = len(pieces)
    rows, width = pieces[0].shape
    hidden = w_gate.shape[1]
    block = width // 7
    vmem = pl.BlockSpec(memory_space=pltpu.VMEM)
    act = pl.pallas_call(
        functools.partial(hidden_body, count=count, block=block),
        out_shape=jax.ShapeDtypeStruct((count * rows, hidden), BF16),
        in_specs=[vmem] * (count + 1) + [pl.BlockSpec(memory_space=pltpu.HBM)],
        out_specs=vmem,
        scratch_shapes=[pltpu.VMEM(w_up.shape, BF16), pltpu.SemaphoreType.DMA((width // block,))],
        compiler_params=pltpu.CompilerParams(vmem_limit_bytes=24 << 20),
    )(*pieces, w_gate, pltpu.with_memory_space_constraint(w_up, pltpu.HBM))
    outs = pl.pallas_call(
        down_body,
        out_shape=[jax.ShapeDtypeStruct((rows, width), BF16)] * count,
        in_specs=[vmem] * 2,
        out_specs=[vmem] * count,
        compiler_params=pltpu.CompilerParams(vmem_limit_bytes=24 << 20),
    )(act, w_down)
    return list(outs)


def join_body(a_ref, b_ref, o_ref):
    o_ref[...] = (a_ref[...].astype(F32) + b_ref[...].astype(F32)).astype(BF16)


def join_kernel(a, b):
    vmem = pl.BlockSpec(memory_space=pltpu.VMEM)
    return pl.pallas_call(
        join_body,
        out_shape=jax.ShapeDtypeStruct(a.shape, BF16),
        in_specs=[vmem, vmem],
        out_specs=vmem,
        compiler_params=pltpu.CompilerParams(vmem_limit_bytes=8 << 20),
    )(a, b)


def shards(tokens, norm_gain, routes, gate_weight, w_gate, w_up, w_down):
    micro, events, width = tokens.shape
    groups = lax.axis_size("node")
    cores = lax.axis_size("core")
    ring_len = lax.axis_size("local")
    sections = lax.axis_size("y") * cores
    total = micro * events
    top = routes.shape[2]
    capacity = min(events, max(2, (events * top + groups - 1) // groups))
    dests = groups * cores
    rows = dests * capacity
    half = ring_len // 2

    pairs = [(s, (s + 1) % sections) for s in range(sections)]
    arrived = lax.ppermute(jnp.transpose(tokens, (1, 0, 2)), ("y", "core"), pairs)
    wide = arrived.astype(F32)
    mean_square = jnp.mean(wide * wide, axis=2, keepdims=True)
    normed = (wide * lax.rsqrt(mean_square + 1e-06) * norm_gain).astype(BF16)
    normed = normed.reshape(total, width)

    chosen = routes[:, :, :, None] == jnp.arange(groups, dtype=jnp.int32)
    picked = jnp.sum(chosen.astype(jnp.int32), axis=2)
    weight = jnp.sum(jnp.where(chosen, gate_weight[:, :, :, None], 0.0), axis=2)
    slot_rank = jnp.cumsum(picked, axis=1) - 1
    placed = (picked[..., None] > 0) & (
        slot_rank[..., None] == jnp.arange(capacity, dtype=jnp.int32)
    )
    ids = jnp.arange(micro)
    want = ids[None, :] ^ ids[:cores, None]
    match = want[:, :, None] == ids
    place = placed[None, None].astype(F32) * match[:, :, :, None, None, None].astype(F32)
    mix = place * weight[None, None, :, :, :, None]
    slots = rows * micro
    place = jnp.transpose(place, (4, 0, 1, 5, 3, 2)).reshape(slots, total)
    mix = jnp.transpose(mix, (4, 0, 1, 5, 3, 2)).reshape(slots, total)

    def exchange(value):
        value = value.reshape(dests, micro * capacity, width)
        return lax.all_to_all(value, ("node", "core"), split_axis=0, concat_axis=0, tiled=True)

    sent = jnp.dot(place.astype(BF16), normed, preferred_element_type=F32)
    got = exchange(sent.astype(BF16)).reshape(dests, micro, capacity, width)
    chains = [[got[:, o].reshape(rows, width)] for o in range(micro)]
    for hop in range(1, half + 1):
        for chain in chains:
            chain.append(ring(chain[-1], 1, hop))

    first, second = chains
    parts = experts(first + second[1:], w_gate[0], w_up[0], w_down[0])
    part_first, part_second = parts[: half + 1], [None] + parts[half + 1 :]

    acc_first, acc_second = part_first[half], part_second[half]
    for hop in range(half, 0, -1):
        acc_first = ring(acc_first, -1, hop)
        if hop > 1:
            acc_first = (acc_first.astype(F32) + part_first[hop - 1].astype(F32)).astype(BF16)
        acc_second = ring(acc_second, -1, hop)
        if hop > 1:
            acc_second = join_kernel(acc_second, part_second[hop - 1])

    back = pack(acc_first, part_first[0], acc_second, dests)
    mixed = lax.dot_general(
        mix,
        exchange(back).reshape(slots, width).astype(F32),
        (((0,), (0,)), ((), ())),
        precision=lax.Precision.HIGHEST,
        preferred_element_type=F32,
    )
    mixed = (wide.reshape(total, width) + mixed).astype(BF16)
    return jnp.transpose(mixed.reshape(events, micro, width), (1, 0, 2))


def solution(mesh):
    sections, nodes, locals_ = mesh.devices.shape
    split = Mesh(
        mesh.devices.reshape(sections // 2, 2, nodes, locals_),
        ("y", "core", "node", "local"),
    )
    spread = ("y", "core", "node", "local")
    placed = (
        P(None, spread, None),
        P(),
        P(None, spread, None),
        P(None, spread, None),
        P("node", None, "local"),
        P("node", None, "local"),
        P("node", "local", None),
    )
    return jax.shard_map(
        shards,
        mesh=split,
        in_specs=placed,
        out_specs=P(None, spread, None),
        check_vma=False,
    )
```
